32 devices in a mesh: shard: 4 (over z), ctx: 4 (over x, core), tensor: 2 (over y).
Axes of the slice: x: 2, y: 2, z: 4, core: 2. Of those that a mesh axis runs over, the one named last changes fastest.
Arguments:
- inputs: bfloat16 [4, 2048, 1024], P('shard', ('ctx', 'tensor')), may hold values from -6 to 6
- ln1_gain: bfloat16 [1024], P(('shard', 'ctx', 'tensor')), may hold values from 0.25 to 1.75
- ln1_bias: bfloat16 [1024], P(('shard', 'ctx', 'tensor')), may hold values from -3 to 3
- ln2_gain: bfloat16 [1024], P(('shard', 'ctx', 'tensor')), may hold values from 0.25 to 1.75
- ln2_bias: bfloat16 [1024], P(('shard', 'ctx', 'tensor')), may hold values from -3 to 3
- w_qkv: bfloat16 [3, 1024, 1024], P(None, ('shard', 'ctx'), 'tensor'), may hold values from -0.1875 to 0.1875
- b_qkv: bfloat16 [3, 2, 512], P(None, 'tensor', ('shard', 'ctx')), may hold values from -3 to 3
- w_out: bfloat16 [1024, 1024], P('tensor', ('shard', 'ctx')), may hold values from -0.75 to 0.75
- b_out: bfloat16 [1024], P(('shard', 'ctx', 'tensor')), may hold values from -3 to 3
- w_up: bfloat16 [1024, 4096], P(('shard', 'ctx'), 'tensor'), may hold values from -0.1875 to 0.1875
- b_up: bfloat16 [2, 2048], P('tensor', ('shard', 'ctx')), may hold values from -3 to 3
- w_down: bfloat16 [4096, 1024], P('tensor', ('shard', 'ctx')), may hold values from -0.09375 to 0.09375
- b_down: bfloat16 [1024], P(('shard', 'ctx', 'tensor')), may hold values from -3 to 3
- cotangent: bfloat16 [4, 2048, 1024], P('shard', ('ctx', 'tensor')), may hold values from -6 to 6
Outputs:
- output: bfloat16 [4, 2048, 1024], P('shard', ('ctx', 'tensor'))
- grad_inputs: float32 [4, 2048, 1024], P('shard', ('ctx', 'tensor'))
- grad_ln1_gain: float32 [1024], P(('shard', 'ctx', 'tensor'))
- grad_ln1_bias: float32 [1024], P(('shard', 'ctx', 'tensor'))
- grad_ln2_gain: float32 [1024], P(('shard', 'ctx', 'tensor'))
- grad_ln2_bias: float32 [1024], P(('shard', 'ctx', 'tensor'))
- grad_w_qkv: float32 [3, 1024, 1024], P(None, ('shard', 'ctx'), 'tensor')
- grad_b_qkv: float32 [3, 2, 512], P(None, 'tensor', ('shard', 'ctx'))
- grad_w_out: float32 [1024, 1024], P('tensor', ('shard', 'ctx'))
- grad_b_out: float32 [1024], P(('shard', 'ctx', 'tensor'))
- grad_w_up: float32 [1024, 4096], P(('shard', 'ctx'), 'tensor')
- grad_b_up: float32 [2, 2048], P('tensor', ('shard', 'ctx'))
- grad_w_down: float32 [4096, 1024], P('tensor', ('shard', 'ctx'))
- grad_b_down: float32 [1024], P(('shard', 'ctx', 'tensor'))
The draws below stay inside these ranges and needn't reach their ends.
All inputs are finite; a program needn't handle non-finite values.
Results may differ from the reference program's by a relative error of at most 0.0097.
Values may be sent and summed in bfloat16 or wider, within the bound.
A program may use at most 128 MiB of HBM per device.

```python
import jax
import jax.numpy as jnp
from jax import lax

D = 1024
H = 16
HD = 64
ROT = 16
FF = 4096
SEQ = 2048
SEQS = 4
N_TENSOR = 2


def block_levels(own_key, dims, shards, least, high):
    def one(axis_at, shards_of):
        draws = jax.random.uniform(jax.random.fold_in(jax.random.fold_in(own_key, 6), axis_at), (shards_of,), jnp.float32, least / len(shards), high / len(shards))
        return jnp.repeat(jnp.exp(draws), dims[axis_at] // shards_of).reshape((-1,) + (1,) * (len(dims) - axis_at - 1))

    level = one(*shards[0])
    for cut in shards[1:]:
        level = level * one(*cut)
    return level


def noise(stream_key, shape, deviation, limit, split=(), kind=jnp.bfloat16):
    values = jax.random.normal(stream_key, shape, jnp.float32) * deviation
    if len(split) > 0:
        values = block_levels(stream_key, shape, split, -0.22, 0.18) * values
    return jnp.clip(values, min=-limit, max=limit).astype(kind)


def setup_inputs(seed: int = 0) -> dict:
    keys = jax.random.split(jax.random.key(seed), 15)
    return {
        "inputs": noise(keys[0], (SEQS, SEQ, D), 1.0, 6.0, ((0, 4), (1, 8))),
        "ln1_gain": jnp.clip(1.0 + 0.15 * jax.random.normal(keys[1], (D,), jnp.float32), 0.25, 1.75).astype(jnp.bfloat16),
        "ln1_bias": noise(keys[2], (D,), 0.5, 3.0, ((0, 32),)),
        "ln2_gain": jnp.clip(1.0 + 0.15 * jax.random.normal(keys[3], (D,), jnp.float32), 0.25, 1.75).astype(jnp.bfloat16),
        "ln2_bias": noise(keys[4], (D,), 0.5, 3.0, ((0, 32),)),
        "w_qkv": noise(keys[5], (3, D, D), D ** -0.5, 0.1875, ((1, 16), (2, 2))),
        "b_qkv": noise(keys[6], (3, N_TENSOR, D // N_TENSOR), 0.5, 3.0, ((1, 2), (2, 16))),
        "w_out": noise(keys[7], (D, D), (D // 16) ** -0.5, 0.75, ((0, 2), (1, 16))),
        "b_out": noise(keys[8], (D,), 0.5, 3.0, ((0, 32),)),
        "w_up": noise(keys[9], (D, FF), D ** -0.5, 0.1875, ((0, 16), (1, 2))),
        "b_up": noise(keys[10], (N_TENSOR, FF // N_TENSOR), 0.5, 3.0, ((0, 2), (1, 16))),
        "w_down": noise(keys[11], (FF, D), FF ** -0.5, 0.09375, ((0, 2), (1, 16))),
        "b_down": noise(keys[12], (D,), 0.5, 3.0, ((0, 32),)),
        "cotangent": noise(keys[13], (SEQS, SEQ, D), 1.0, 6.0, ((0, 4), (1, 8))),
    }


norm_eps = 1e-05
rope_base = 10000.0
highest = lax.Precision.HIGHEST

@jax.custom_vjp
def low(v):
    return lax.optimization_barrier(v.astype(jnp.bfloat16)).astype(jnp.float32)

@jax.custom_vjp
def low_back(v):
    return v

def low_keep(v):
    return (low(v), None)

def low_pass(kept, grad):
    return (grad,)

def back_keep(v):
    return (v, None)

def back_low(kept, grad):
    return (low(grad),)
low.defvjp(low_keep, low_pass)
low_back.defvjp(back_keep, back_low)

def layer_norm(values, gain, shift):
    centre = values - lax.optimization_barrier(jnp.mean(values, -1, keepdims=True))
    spread = lax.optimization_barrier(jnp.mean(centre * centre, -1, keepdims=True))
    return centre * lax.rsqrt(spread + norm_eps) * gain + shift

def rotary_tables(positions):
    half_dims = ROT // 2
    ladder = jnp.arange(half_dims, dtype=jnp.float32)
    inverse = jnp.exp(ladder * (-2.0 / ROT) * jnp.log(jnp.float32(rope_base)))
    angles = positions.astype(jnp.float32)[:, None] * inverse[None, :]
    angles = jnp.concatenate([angles, angles], -1)
    return (jnp.cos(angles)[:, None, :], jnp.sin(angles)[:, None, :])

def rotate(values, cosine, sine_table):
    rot_dims = cosine.shape[-1]
    half_dims = rot_dims // 2
    turned = values[..., :rot_dims]
    swapped = jnp.concatenate([-turned[..., half_dims:], turned[..., :half_dims]], -1)
    return jnp.concatenate([turned * cosine + swapped * sine_table, values[..., rot_dims:]], -1)

def layer_forward(params, values):
    ln1_gain, ln1_bias, ln2_gain, ln2_bias, w_qkv, b_qkv, w_out, b_out, w_up, b_up, w_down, b_down = params
    first_norm = low(layer_norm(values, ln1_gain, ln1_bias))
    second_norm = low(layer_norm(values, ln2_gain, ln2_bias))
    projected = jnp.einsum('sd,jde->jse', first_norm, w_qkv, precision=highest) + b_qkv.reshape(3, 1, D)
    projected = low_back(projected)
    cosine, sine_table = rotary_tables(jnp.arange(SEQ, dtype=jnp.int32))
    queries = low(low_back(rotate(projected[0].reshape(SEQ, H, HD), cosine, sine_table)))
    key_rows = low(low_back(rotate(projected[1].reshape(SEQ, H, HD), cosine, sine_table)))
    value_rows = low(projected[2].reshape(SEQ, H, HD))
    block_rows = min(512, SEQ)
    block_count = SEQ // block_rows
    score_scale = HD ** (-0.5)
    key_pos = jnp.arange(SEQ, dtype=jnp.int32)

    def attend_block(block_pack):
        query_block, offset = block_pack
        scores = jnp.einsum('qhd,khd->hqk', query_block, key_rows, precision=highest) * score_scale
        scores = low_back(scores)
        causal = key_pos[None, :] <= (offset + jnp.arange(block_rows, dtype=jnp.int32))[:, None]
        scores = jnp.where(causal[None], scores, -1e+30)
        attn_prob = low(jax.nn.softmax(scores, -1))
        return jnp.einsum('hqk,khd->qhd', attn_prob, value_rows, precision=highest)
    offsets = jnp.arange(block_count, dtype=jnp.int32) * block_rows
    mixed_blocks = lax.map(jax.checkpoint(attend_block), (queries.reshape(block_count, block_rows, H, HD), offsets))
    heads_out = low_back(low(mixed_blocks.reshape(SEQ, D)))
    attention = jnp.dot(heads_out, w_out, precision=highest) + b_out
    hidden_pre = low_back(jnp.dot(second_norm, w_up, precision=highest) + b_up.reshape(FF))
    hidden = low(jax.nn.gelu(hidden_pre, approximate=False))
    feed_out = jnp.dot(hidden, w_down, precision=highest) + b_down
    return values + attention + feed_out

def reference(inputs, ln1_gain, ln1_bias, ln2_gain, ln2_bias, w_qkv, b_qkv, w_out, b_out, w_up, b_up, w_down, b_down, cotangent):
    params = tuple((weight.astype(jnp.float32) for weight in (ln1_gain, ln1_bias, ln2_gain, ln2_bias, w_qkv, b_qkv, w_out, b_out, w_up, b_up, w_down, b_down)))

    def one_sequence(totals, seq_pair):
        seq_in, seq_cot = seq_pair
        result, pullback = jax.vjp(layer_forward, params, seq_in.astype(jnp.float32))
        param_grads, input_grad = pullback(seq_cot.astype(jnp.float32))
        totals = jax.tree.map(lambda running, update: running + update, totals, param_grads)
        return (totals, (result.astype(jnp.bfloat16), input_grad))
    zero_state = jax.tree.map(jnp.zeros_like, params)
    totals, (outputs, input_grads) = lax.scan(one_sequence, zero_state, (inputs, cotangent))
    return (outputs, input_grads, totals[0], totals[1], totals[2], totals[3], totals[4], totals[5], totals[6], totals[7], totals[8], totals[9], totals[10], totals[11])
```

```python
import functools

import jax
import jax.numpy as jnp
from jax import lax
from jax.experimental import pallas as pl
from jax.experimental.pallas import tpu as pltpu
from jax.sharding import PartitionSpec as P

HD = 64
ROT = 16


norm_eps = 1e-05
rope_base = 10000.0
bf16 = jnp.bfloat16
f32 = jnp.float32
GROUP = ("shard", "ctx")


def layer_norm_parts(values):
    centre = values - jnp.mean(values, -1, keepdims=True)
    spread = jnp.mean(centre * centre, -1, keepdims=True)
    inv_std = lax.rsqrt(spread + norm_eps)
    return (centre * inv_std, inv_std)


def rotary_tables(positions):
    half_dims = ROT // 2
    ladder = jnp.arange(half_dims, dtype=f32)
    inverse = jnp.exp(ladder * (-2.0 / ROT) * jnp.log(f32(rope_base)))
    angles = positions.astype(f32)[:, None] * inverse[None, :]
    angles = jnp.concatenate([angles, angles], -1)
    return (jnp.cos(angles)[:, None, :], jnp.sin(angles)[:, None, :])


def rotate(values, cosine, sine_table):
    rot_dims = cosine.shape[-1]
    half_dims = rot_dims // 2
    turned = values[..., :rot_dims]
    swapped = jnp.concatenate([-turned[..., half_dims:], turned[..., :half_dims]], -1)
    return jnp.concatenate([turned * cosine + swapped * sine_table, values[..., rot_dims:]], -1)


def gelu_slope(values):
    return (
        0.5 * (1.0 + lax.erf(values * 0.7071067811865476))
        + values * jnp.exp(-0.5 * values * values) * 0.3989422804014327
    )


def contract_last(left_side, right_side):
    return lax.dot_general(
        left_side, right_side, (((1,), (1,)), ((), ())), preferred_element_type=f32
    )


def contract_first(left_side, right_side):
    return lax.dot_general(
        left_side, right_side, (((0,), (0,)), ((), ())), preferred_element_type=f32
    )


def attention_kernel(lanes, wide, rows, in_ref, out_ref, key_grad, value_grad):
    seq_len = in_ref.shape[0]
    heads = lanes // HD
    parts = wide // rows
    scale = HD ** (-0.5)
    key_grad[...] = jnp.zeros_like(key_grad)
    value_grad[...] = jnp.zeros_like(value_grad)
    out_ref[...] = jnp.zeros_like(out_ref)
    for step in range(seq_len // wide):
        length = (step + 1) * wide

        def one_block(turn, carry, step=step, length=length):
            head = turn % heads
            start = pl.multiple_of(step * wide + (turn // heads) * rows, rows)
            here = pl.ds(start, rows)
            mine = lax.broadcasted_iota(jnp.int32, (rows, lanes), 1) // HD == head
            queries = in_ref[here, 0:lanes].astype(f32) * scale
            queries = jnp.where(mine, queries, 0.0).astype(bf16)
            grads = in_ref[here, 3 * lanes : 4 * lanes].astype(f32)
            grads = jnp.where(mine, grads, 0.0).astype(bf16)
            keys = in_ref[0:length, lanes : 2 * lanes]
            values = in_ref[0:length, 2 * lanes : 3 * lanes]
            scores = contract_last(queries, keys)
            key_at = lax.broadcasted_iota(jnp.int32, scores.shape, 1)
            query_at = start + lax.broadcasted_iota(jnp.int32, scores.shape, 0)
            scores = jnp.where(key_at <= query_at, scores, -1e30)
            exp_scores = jnp.exp(scores - jnp.max(scores, -1, keepdims=True))
            probs = exp_scores * (1.0 / jnp.sum(exp_scores, -1, keepdims=True))
            attn_prob = probs.astype(bf16)
            mixed = jnp.dot(attn_prob, values, preferred_element_type=f32)
            value_grad[0:length, :] += contract_first(attn_prob, grads)
            prob_grad = contract_last(grads, values)
            inner_sum = jnp.sum(probs * prob_grad, -1, keepdims=True)
            score_grad = (probs * (prob_grad - inner_sum)).astype(bf16)
            query_grad = jnp.dot(score_grad, keys, preferred_element_type=f32) * scale
            key_grad[0:length, :] += contract_first(score_grad, queries)
            out_ref[here, 0:lanes] = jnp.where(
                mine, mixed, out_ref[here, 0:lanes].astype(f32)
            ).astype(bf16)
            out_ref[here, lanes : 2 * lanes] = jnp.where(
                mine, query_grad, out_ref[here, lanes : 2 * lanes].astype(f32)
            ).astype(bf16)
            return carry

        lax.fori_loop(0, parts * heads, one_block, 0)
    out_ref[:, 2 * lanes : 3 * lanes] = key_grad[...].astype(bf16)
    out_ref[:, 3 * lanes : 4 * lanes] = value_grad[...].astype(bf16)


def attend(packed):
    seq_len, width = packed.shape
    lanes = width // 4
    wide = min(512, seq_len)
    rows = min(256, wide)
    return pl.pallas_call(
        functools.partial(attention_kernel, lanes, wide, rows),
        out_shape=jax.ShapeDtypeStruct((seq_len, width), bf16),
        in_specs=[pl.BlockSpec(memory_space=pltpu.VMEM)],
        out_specs=pl.BlockSpec(memory_space=pltpu.VMEM),
        scratch_shapes=[pltpu.VMEM((seq_len, lanes), f32), pltpu.VMEM((seq_len, lanes), f32)],
        compiler_params=pltpu.CompilerParams(vmem_limit_bytes=48 << 20),
        cost_estimate=pl.CostEstimate(
            flops=14 * seq_len * seq_len * lanes,
            bytes_accessed=4 * seq_len * width,
            transcendentals=seq_len * seq_len * lanes // HD,
        ),
    )(packed)


def per_device(
    inputs,
    ln1_gain,
    ln1_bias,
    ln2_gain,
    ln2_bias,
    w_qkv,
    b_qkv,
    w_out,
    b_out,
    w_up,
    b_up,
    w_down,
    b_down,
    cotangent,
):
    pair = lax.axis_index("tensor")
    first = pair == 0
    n_ctx = lax.axis_size("ctx")
    n_group = lax.axis_size("shard") * n_ctx
    swap = ((0, 1), (1, 0))

    def exchange(value):
        return lax.ppermute(value, "tensor", swap)

    def in_order(own, other, axis):
        return jnp.where(
            first,
            jnp.concatenate([own, other], axis),
            jnp.concatenate([other, own], axis),
        )

    small_own = jnp.stack([ln1_gain, ln1_bias, ln2_gain, ln2_bias, b_out, b_down])
    small = in_order(small_own, exchange(small_own), 1)
    piece = small.shape[1]
    depth = w_up.shape[0]
    ff_group = w_up.shape[1]
    width = w_qkv.shape[2]
    riders = jnp.concatenate([small.reshape(-1), b_qkv.reshape(-1), b_up.reshape(-1)])
    room = depth * 128
    riders = jnp.pad(riders, (0, room - riders.shape[0])).reshape(depth, 128)
    first_pack = jnp.concatenate([w_qkv[0], w_qkv[1], w_qkv[2], w_out.T, riders], 1)
    second_pack = jnp.concatenate([w_up, w_down.T], 1)
    first_whole = lax.all_gather(first_pack, GROUP, axis=0, tiled=True)
    second_whole = lax.all_gather(second_pack, GROUP, axis=0, tiled=True)
    model = first_whole.shape[0]
    whole_qkv = first_whole[:, : 3 * width]
    whole_out_t = first_whole[:, 3 * width : 4 * width]
    gathered = first_whole[:, 4 * width :].reshape(n_group, room).astype(f32)
    whole_up = second_whole[:, :ff_group]
    whole_down_t = second_whole[:, ff_group:]

    gain_one, shift_one, gain_two, shift_two, bias_out, bias_down = [
        gathered[:, at * piece : (at + 1) * piece].reshape(-1) for at in range(6)
    ]
    at = 6 * piece
    part = b_qkv.shape[2]
    bias_qkv = jnp.concatenate(
        [gathered[:, at + j * part : at + (j + 1) * part].reshape(-1) for j in range(3)]
    )
    at = at + 3 * part
    up_part = b_up.shape[1]
    bias_up = gathered[:, at : at + up_part].reshape(-1)

    both_own = jnp.concatenate([inputs, cotangent], 0)
    both = in_order(both_own, exchange(both_own), 1)
    grad_own = cotangent[0]
    own_rows = inputs[0].astype(f32)
    normed_own, inv_own = layer_norm_parts(own_rows)
    normed, _ = layer_norm_parts(both[0].astype(f32))
    grad_rows = both[1]
    first_norm = (normed * gain_one + shift_one).astype(bf16)
    second_norm = (normed * gain_two + shift_two).astype(bf16)
    block_len = first_norm.shape[0]
    half = block_len // 2

    def own_half(value):
        return jnp.where(first, value[:half], value[half:])

    def other_half(value):
        return jnp.where(first, value[half:], value[:half])

    positions = lax.axis_index("ctx") * block_len + jnp.arange(block_len, dtype=jnp.int32)
    cosine, sine_table = rotary_tables(positions)
    projected = jnp.dot(first_norm, whole_qkv, preferred_element_type=f32) + bias_qkv
    heads = width // HD

    def turned(value, sine):
        return (
            rotate(value.astype(f32).reshape(block_len, heads, HD), cosine, sine)
            .astype(bf16)
            .reshape(block_len, width)
        )

    queries = turned(projected[:, :width], sine_table)
    key_rows = turned(projected[:, width : 2 * width], sine_table)
    value_rows = projected[:, 2 * width :].astype(bf16)
    grad_mixed = jnp.dot(grad_rows, whole_out_t, preferred_element_type=f32).astype(bf16)
    lanes = width // n_ctx
    packed = jnp.stack([queries, key_rows, value_rows, grad_mixed])
    packed = packed.reshape(4, block_len, n_ctx, lanes).transpose(2, 1, 0, 3)
    packed = packed.reshape(n_ctx, block_len, 4 * lanes)

    hidden_pre = jnp.dot(second_norm, whole_up, preferred_element_type=f32) + bias_up
    hidden = jax.nn.gelu(hidden_pre, approximate=False).astype(bf16)
    feed_out = contract_last(hidden, whole_down_t)
    grad_hidden = jnp.dot(grad_rows, whole_down_t, preferred_element_type=f32)
    grad_pre = (grad_hidden * gelu_slope(hidden_pre)).astype(bf16)
    grad_up = contract_first(second_norm, grad_pre).astype(bf16)
    grad_down_t = contract_first(grad_rows, hidden).astype(bf16)
    second_grads = jnp.concatenate([grad_up, grad_down_t], 1)
    packed, second_grads = lax.optimization_barrier((packed, second_grads))
    second_sum = lax.psum_scatter(second_grads, GROUP, scatter_dimension=0, tiled=True)
    grad_b_up = jnp.sum(grad_pre, 0, dtype=f32)
    grad_second = contract_last(grad_pre, whole_up)

    there = lax.all_to_all(packed, "ctx", split_axis=0, concat_axis=0, tiled=True)
    attended = attend(there.reshape(n_ctx * block_len, 4 * lanes))
    back = lax.all_to_all(
        attended.reshape(n_ctx, block_len, 4 * lanes),
        "ctx",
        split_axis=0,
        concat_axis=0,
        tiled=True,
    )
    back = back.reshape(n_ctx, block_len, 4, lanes).transpose(2, 1, 0, 3)
    mixed_rows, query_back, key_back, value_back = back.reshape(4, block_len, width)
    grad_projected = jnp.concatenate(
        [turned(query_back, -sine_table), turned(key_back, -sine_table), value_back], 1
    )
    grad_qkv = contract_first(first_norm, grad_projected).astype(bf16)
    grad_out_t = contract_first(grad_rows, mixed_rows).astype(bf16)
    grad_b_qkv = jnp.sum(grad_projected, 0, dtype=f32)
    grad_first = contract_last(grad_projected, whole_qkv)

    vectors = jnp.stack(
        [
            jnp.sum(grad_first * normed, 0),
            jnp.sum(grad_first, 0),
            jnp.sum(grad_second * normed, 0),
            jnp.sum(grad_second, 0),
            jnp.sum(grad_own.astype(f32), 0),
        ]
    )
    back_riders = jnp.concatenate(
        [
            vectors.reshape(5, n_group, piece).transpose(1, 0, 2).reshape(n_group, -1),
            grad_b_qkv.reshape(3, n_group, part).transpose(1, 0, 2).reshape(n_group, -1),
            grad_b_up.reshape(n_group, up_part),
        ],
        1,
    )
    back_riders = jnp.pad(back_riders, ((0, 0), (0, room - back_riders.shape[1])))
    back_riders = back_riders.reshape(model, 128).astype(bf16)
    first_grads = jnp.concatenate([grad_qkv, grad_out_t, back_riders], 1)
    first_sum = lax.psum_scatter(first_grads, GROUP, scatter_dimension=0, tiled=True)

    partial_sum = contract_last(mixed_rows, whole_out_t) + feed_out
    branches = own_half(partial_sum) + exchange(other_half(partial_sum).astype(bf16)).astype(f32)
    output = (own_rows + branches + bias_out + bias_down).astype(bf16)
    scaled = grad_first * gain_one + grad_second * gain_two
    scaled = own_half(scaled) + exchange(other_half(scaled).astype(bf16)).astype(f32)
    inner_sum = jnp.mean(scaled, -1, keepdims=True)
    aligned = jnp.mean(scaled * normed_own, -1, keepdims=True)
    grad_input = grad_own.astype(f32) + inv_own * (scaled - inner_sum - normed_own * aligned)

    second_sum = second_sum.astype(f32)
    first_sum = first_sum.astype(f32)
    grad_w_qkv = first_sum[:, : 3 * width].reshape(depth, 3, width).transpose(1, 0, 2)
    grad_w_out = first_sum[:, 3 * width : 4 * width].T
    summed = first_sum[:, 4 * width :].reshape(-1)
    vector_sum = summed[: 5 * piece].reshape(5, piece)
    own = piece // 2
    mine = jnp.where(first, vector_sum[:, :own], vector_sum[:, own:])
    theirs = jnp.where(first, vector_sum[:, own:], vector_sum[:, :own])
    vector_grads = mine + exchange(theirs)
    at = 5 * piece
    out_b_qkv = summed[at : at + 3 * part].reshape(3, 1, part)
    at = at + 3 * part
    out_b_up = summed[at : at + up_part].reshape(1, up_part)
    return (
        output[None],
        grad_input[None],
        vector_grads[0],
        vector_grads[1],
        vector_grads[2],
        vector_grads[3],
        grad_w_qkv,
        out_b_qkv,
        grad_w_out,
        vector_grads[4],
        second_sum[:, :ff_group],
        out_b_up,
        second_sum[:, ff_group:].T,
        vector_grads[4],
    )


def solution(mesh):
    placed = (
        P("shard", ("ctx", "tensor"), None),
        P(("shard", "ctx", "tensor")),
        P(("shard", "ctx", "tensor")),
        P(("shard", "ctx", "tensor")),
        P(("shard", "ctx", "tensor")),
        P(None, ("shard", "ctx"), "tensor"),
        P(None, "tensor", ("shard", "ctx")),
        P("tensor", ("shard", "ctx")),
        P(("shard", "ctx", "tensor")),
        P(("shard", "ctx"), "tensor"),
        P("tensor", ("shard", "ctx")),
        P("tensor", ("shard", "ctx")),
        P(("shard", "ctx", "tensor")),
        P("shard", ("ctx", "tensor"), None),
    )
    return jax.shard_map(
        per_device,
        mesh=mesh,
        in_specs=placed,
        out_specs=(
            P("shard", ("ctx", "tensor"), None),
            P("shard", ("ctx", "tensor"), None),
            P(("shard", "ctx", "tensor")),
            P(("shard", "ctx", "tensor")),
            P(("shard", "ctx", "tensor")),
            P(("shard", "ctx", "tensor")),
            P(None, ("shard", "ctx"), "tensor"),
            P(None, "tensor", ("shard", "ctx")),
            P("tensor", ("shard", "ctx")),
            P(("shard", "ctx", "tensor")),
            P(("shard", "ctx"), "tensor"),
            P("tensor", ("shard", "ctx")),
            P("tensor", ("shard", "ctx")),
            P(("shard", "ctx", "tensor")),
        ),
        check_vma=False,
    )
```

```python
import functools

import jax
import jax.numpy as jnp
from jax import lax
from jax.experimental import pallas as pl
from jax.experimental.pallas import tpu as pltpu
from jax.sharding import PartitionSpec as P

HD = 64
ROT = 16


norm_eps = 1e-05
rope_base = 10000.0
bf16 = jnp.bfloat16
f32 = jnp.float32
GROUP = ("shard", "ctx")


def layer_norm_parts(values):
    centre = values - jnp.mean(values, -1, keepdims=True)
    spread = jnp.mean(centre * centre, -1, keepdims=True)
    inv_std = lax.rsqrt(spread + norm_eps)
    return (centre * inv_std, inv_std)


def rotary_tables(positions):
    half_dims = ROT // 2
    ladder = jnp.arange(half_dims, dtype=f32)
    inverse = jnp.exp(ladder * (-2.0 / ROT) * jnp.log(f32(rope_base)))
    angles = positions.astype(f32)[:, None] * inverse[None, :]
    angles = jnp.concatenate([angles, angles], -1)
    return (jnp.cos(angles)[:, None, :], jnp.sin(angles)[:, None, :])


def rotate(values, cosine, sine_table):
    rot_dims = cosine.shape[-1]
    half_dims = rot_dims // 2
    turned = values[..., :rot_dims]
    swapped = jnp.concatenate([-turned[..., half_dims:], turned[..., :half_dims]], -1)
    return jnp.concatenate([turned * cosine + swapped * sine_table, values[..., rot_dims:]], -1)


def gelu_slope(values):
    return (
        0.5 * (1.0 + lax.erf(values * 0.7071067811865476))
        + values * jnp.exp(-0.5 * values * values) * 0.3989422804014327
    )


def contract_last(left_side, right_side):
    return lax.dot_general(
        left_side, right_side, (((1,), (1,)), ((), ())), preferred_element_type=f32
    )


def contract_first(left_side, right_side):
    return lax.dot_general(
        left_side, right_side, (((0,), (0,)), ((), ())), preferred_element_type=f32
    )


def attention_kernel(lanes, wide, rows, in_ref, out_ref, key_grad, value_grad):
    seq_len = in_ref.shape[0]
    heads = lanes // HD
    parts = wide // rows
    scale = HD ** (-0.5)
    key_grad[...] = jnp.zeros_like(key_grad)
    value_grad[...] = jnp.zeros_like(value_grad)
    out_ref[...] = jnp.zeros_like(out_ref)
    for step in range(seq_len // wide):
        length = (step + 1) * wide

        def one_block(turn, carry, step=step, length=length):
            head = turn % heads
            start = pl.multiple_of(step * wide + (turn // heads) * rows, rows)
            here = pl.ds(start, rows)
            mine = lax.broadcasted_iota(jnp.int32, (rows, lanes), 1) // HD == head
            queries = in_ref[here, 0:lanes].astype(f32) * scale
            queries = jnp.where(mine, queries, 0.0).astype(bf16)
            grads = in_ref[here, 3 * lanes : 4 * lanes].astype(f32)
            grads = jnp.where(mine, grads, 0.0).astype(bf16)
            keys = in_ref[0:length, lanes : 2 * lanes]
            values = in_ref[0:length, 2 * lanes : 3 * lanes]
            scores = contract_last(queries, keys)
            key_at = lax.broadcasted_iota(jnp.int32, scores.shape, 1)
            query_at = start + lax.broadcasted_iota(jnp.int32, scores.shape, 0)
            scores = jnp.where(key_at <= query_at, scores, -1e30)
            exp_scores = jnp.exp(scores - jnp.max(scores, -1, keepdims=True))
            probs = exp_scores * (1.0 / jnp.sum(exp_scores, -1, keepdims=True))
            attn_prob = probs.astype(bf16)
            mixed = jnp.dot(attn_prob, values, preferred_element_type=f32)
            value_grad[0:length, :] += contract_first(attn_prob, grads)
            prob_grad = contract_last(grads, values)
            inner_sum = jnp.sum(probs * prob_grad, -1, keepdims=True)
            score_grad = (probs * (prob_grad - inner_sum)).astype(bf16)
            query_grad = jnp.dot(score_grad, keys, preferred_element_type=f32) * scale
            key_grad[0:length, :] += contract_first(score_grad, queries)
            out_ref[here, 0:lanes] = jnp.where(
                mine, mixed, out_ref[here, 0:lanes].astype(f32)
            ).astype(bf16)
            out_ref[here, lanes : 2 * lanes] = jnp.where(
                mine, query_grad, out_ref[here, lanes : 2 * lanes].astype(f32)
            ).astype(bf16)
            return carry

        lax.fori_loop(0, parts * heads, one_block, 0)
    out_ref[:, 2 * lanes : 3 * lanes] = key_grad[...].astype(bf16)
    out_ref[:, 3 * lanes : 4 * lanes] = value_grad[...].astype(bf16)


def attend(packed):
    seq_len, width = packed.shape
    lanes = width // 4
    wide = min(512, seq_len)
    rows = min(256, wide)
    return pl.pallas_call(
        functools.partial(attention_kernel, lanes, wide, rows),
        out_shape=jax.ShapeDtypeStruct((seq_len, width), bf16),
        in_specs=[pl.BlockSpec(memory_space=pltpu.VMEM)],
        out_specs=pl.BlockSpec(memory_space=pltpu.VMEM),
        scratch_shapes=[pltpu.VMEM((seq_len, lanes), f32), pltpu.VMEM((seq_len, lanes), f32)],
        compiler_params=pltpu.CompilerParams(vmem_limit_bytes=48 << 20),
        cost_estimate=pl.CostEstimate(
            flops=14 * seq_len * seq_len * lanes,
            bytes_accessed=4 * seq_len * width,
            transcendentals=seq_len * seq_len * lanes // HD,
        ),
    )(packed)


def per_device(
    inputs,
    ln1_gain,
    ln1_bias,
    ln2_gain,
    ln2_bias,
    w_qkv,
    b_qkv,
    w_out,
    b_out,
    w_up,
    b_up,
    w_down,
    b_down,
    cotangent,
):
    pair = lax.axis_index("tensor")
    first = pair == 0
    n_ctx = lax.axis_size("ctx")
    n_group = lax.axis_size("shard") * n_ctx
    swap = ((0, 1), (1, 0))

    def exchange(value):
        return lax.ppermute(value, "tensor", swap)

    def in_order(own, other, axis):
        return jnp.where(
            first,
            jnp.concatenate([own, other], axis),
            jnp.concatenate([other, own], axis),
        )

    small_own = jnp.stack([ln1_gain, ln1_bias, ln2_gain, ln2_bias, b_out, b_down])
    small = in_order(small_own, exchange(small_own), 1)
    piece = small.shape[1]
    depth = w_up.shape[0]
    ff_group = w_up.shape[1]
    width = w_qkv.shape[2]
    riders = jnp.concatenate([small.reshape(-1), b_qkv.reshape(-1), b_up.reshape(-1)])
    room = depth * 128
    riders = jnp.pad(riders, (0, room - riders.shape[0])).reshape(depth, 128)
    first_pack = jnp.concatenate([w_qkv[0], w_qkv[1], w_qkv[2], w_out.T, riders], 1)
    second_pack = jnp.concatenate([w_up, w_down.T], 1)
    first_whole = lax.all_gather(first_pack, GROUP, axis=0, tiled=True)
    second_whole = lax.all_gather(second_pack, GROUP, axis=0, tiled=True)
    model = first_whole.shape[0]
    whole_qkv = first_whole[:, : 3 * width]
    whole_out_t = first_whole[:, 3 * width : 4 * width]
    gathered = first_whole[:, 4 * width :].reshape(n_group, room).astype(f32)
    whole_up = second_whole[:, :ff_group]
    whole_down_t = second_whole[:, ff_group:]

    gain_one, shift_one, gain_two, shift_two, bias_out, bias_down = [
        gathered[:, at * piece : (at + 1) * piece].reshape(-1) for at in range(6)
    ]
    at = 6 * piece
    part = b_qkv.shape[2]
    bias_qkv = jnp.concatenate(
        [gathered[:, at + j * part : at + (j + 1) * part].reshape(-1) for j in range(3)]
    )
    at = at + 3 * part
    up_part = b_up.shape[1]
    bias_up = gathered[:, at : at + up_part].reshape(-1)

    both_own = jnp.concatenate([inputs, cotangent], 0)
    both = in_order(both_own, exchange(both_own), 1)
    grad_own = cotangent[0]
    own_rows = inputs[0].astype(f32)
    normed_own, inv_own = layer_norm_parts(own_rows)
    normed, _ = layer_norm_parts(both[0].astype(f32))
    grad_rows = both[1]
    first_norm = (normed * gain_one + shift_one).astype(bf16)
    second_norm = (normed * gain_two + shift_two).astype(bf16)
    block_len = first_norm.shape[0]
    half = block_len // 2

    def own_half(value):
        return jnp.where(first, value[:half], value[half:])

    def other_half(value):
        return jnp.where(first, value[half:], value[:half])

    positions = lax.axis_index("ctx") * block_len + jnp.arange(block_len, dtype=jnp.int32)
    cosine, sine_table = rotary_tables(positions)
    projected = jnp.dot(first_norm, whole_qkv, preferred_element_type=f32) + bias_qkv
    heads = width // HD

    def turned(value, sine):
        return (
            rotate(value.astype(f32).reshape(block_len, heads, HD), cosine, sine)
            .astype(bf16)
            .reshape(block_len, width)
        )

    queries = turned(projected[:, :width], sine_table)
    key_rows = turned(projected[:, width : 2 * width], sine_table)
    value_rows = projected[:, 2 * width :].astype(bf16)
    grad_mixed = jnp.dot(grad_rows, whole_out_t, preferred_element_type=f32).astype(bf16)
    lanes = width // n_ctx
    packed = jnp.stack([queries, key_rows, value_rows, grad_mixed])
    packed = packed.reshape(4, block_len, n_ctx, lanes).transpose(2, 1, 0, 3)
    packed = packed.reshape(n_ctx, block_len, 4 * lanes)
    there = lax.all_to_all(packed, "ctx", split_axis=0, concat_axis=0, tiled=True)

    hidden_pre = jnp.dot(second_norm, whole_up, preferred_element_type=f32) + bias_up
    hidden = jax.nn.gelu(hidden_pre, approximate=False).astype(bf16)
    feed_out = contract_last(hidden, whole_down_t)
    grad_hidden = jnp.dot(grad_rows, whole_down_t, preferred_element_type=f32)
    grad_pre = (grad_hidden * gelu_slope(hidden_pre)).astype(bf16)
    grad_up = contract_first(second_norm, grad_pre).astype(bf16)
    grad_down_t = contract_first(grad_rows, hidden).astype(bf16)
    second_grads = jnp.concatenate([grad_up, grad_down_t], 1)
    there, second_grads = lax.optimization_barrier((there, second_grads))
    second_sum = lax.psum_scatter(second_grads, GROUP, scatter_dimension=0, tiled=True)
    grad_b_up = jnp.sum(grad_pre, 0, dtype=f32)
    grad_second = contract_last(grad_pre, whole_up)

    attended = attend(there.reshape(n_ctx * block_len, 4 * lanes))
    back = lax.all_to_all(
        attended.reshape(n_ctx, block_len, 4 * lanes),
        "ctx",
        split_axis=0,
        concat_axis=0,
        tiled=True,
    )
    back = back.reshape(n_ctx, block_len, 4, lanes).transpose(2, 1, 0, 3)
    mixed_rows, query_back, key_back, value_back = back.reshape(4, block_len, width)
    grad_projected = jnp.concatenate(
        [turned(query_back, -sine_table), turned(key_back, -sine_table), value_back], 1
    )
    grad_qkv = contract_first(first_norm, grad_projected).astype(bf16)
    grad_out_t = contract_first(grad_rows, mixed_rows).astype(bf16)
    grad_b_qkv = jnp.sum(grad_projected, 0, dtype=f32)
    grad_first = contract_last(grad_projected, whole_qkv)

    vectors = jnp.stack(
        [
            jnp.sum(grad_first * normed, 0),
            jnp.sum(grad_first, 0),
            jnp.sum(grad_second * normed, 0),
            jnp.sum(grad_second, 0),
            jnp.sum(grad_own.astype(f32), 0),
        ]
    )
    back_riders = jnp.concatenate(
        [
            vectors.reshape(5, n_group, piece).transpose(1, 0, 2).reshape(n_group, -1),
            grad_b_qkv.reshape(3, n_group, part).transpose(1, 0, 2).reshape(n_group, -1),
            grad_b_up.reshape(n_group, up_part),
        ],
        1,
    )
    back_riders = jnp.pad(back_riders, ((0, 0), (0, room - back_riders.shape[1])))
    back_riders = back_riders.reshape(model, 128).astype(bf16)
    first_grads = jnp.concatenate([grad_qkv, grad_out_t, back_riders], 1)
    first_grads, second_sum = lax.optimization_barrier((first_grads, second_sum))
    first_sum = lax.psum_scatter(first_grads, GROUP, scatter_dimension=0, tiled=True)

    partial_sum = contract_last(mixed_rows, whole_out_t) + feed_out
    branches = own_half(partial_sum) + exchange(other_half(partial_sum).astype(bf16)).astype(f32)
    output = (own_rows + branches + bias_out + bias_down).astype(bf16)
    scaled = grad_first * gain_one + grad_second * gain_two
    scaled = own_half(scaled) + exchange(other_half(scaled).astype(bf16)).astype(f32)
    inner_sum = jnp.mean(scaled, -1, keepdims=True)
    aligned = jnp.mean(scaled * normed_own, -1, keepdims=True)
    grad_input = grad_own.astype(f32) + inv_own * (scaled - inner_sum - normed_own * aligned)

    second_sum = second_sum.astype(f32)
    first_sum = first_sum.astype(f32)
    grad_w_qkv = first_sum[:, : 3 * width].reshape(depth, 3, width).transpose(1, 0, 2)
    grad_w_out = first_sum[:, 3 * width : 4 * width].T
    summed = first_sum[:, 4 * width :].reshape(-1)
    vector_sum = summed[: 5 * piece].reshape(5, piece)
    own = piece // 2
    mine = jnp.where(first, vector_sum[:, :own], vector_sum[:, own:])
    theirs = jnp.where(first, vector_sum[:, own:], vector_sum[:, :own])
    vector_grads = mine + exchange(theirs)
    at = 5 * piece
    out_b_qkv = summed[at : at + 3 * part].reshape(3, 1, part)
    at = at + 3 * part
    out_b_up = summed[at : at + up_part].reshape(1, up_part)
    return (
        output[None],
        grad_input[None],
        vector_grads[0],
        vector_grads[1],
        vector_grads[2],
        vector_grads[3],
        grad_w_qkv,
        out_b_qkv,
        grad_w_out,
        vector_grads[4],
        second_sum[:, :ff_group],
        out_b_up,
        second_sum[:, ff_group:].T,
        vector_grads[4],
    )


def solution(mesh):
    placed = (
        P("shard", ("ctx", "tensor"), None),
        P(("shard", "ctx", "tensor")),
        P(("shard", "ctx", "tensor")),
        P(("shard", "ctx", "tensor")),
        P(("shard", "ctx", "tensor")),
        P(None, ("shard", "ctx"), "tensor"),
        P(None, "tensor", ("shard", "ctx")),
        P("tensor", ("shard", "ctx")),
        P(("shard", "ctx", "tensor")),
        P(("shard", "ctx"), "tensor"),
        P("tensor", ("shard", "ctx")),
        P("tensor", ("shard", "ctx")),
        P(("shard", "ctx", "tensor")),
        P("shard", ("ctx", "tensor"), None),
    )
    return jax.shard_map(
        per_device,
        mesh=mesh,
        in_specs=placed,
        out_specs=(
            P("shard", ("ctx", "tensor"), None),
            P("shard", ("ctx", "tensor"), None),
            P(("shard", "ctx", "tensor")),
            P(("shard", "ctx", "tensor")),
            P(("shard", "ctx", "tensor")),
            P(("shard", "ctx", "tensor")),
            P(None, ("shard", "ctx"), "tensor"),
            P(None, "tensor", ("shard", "ctx")),
            P("tensor", ("shard", "ctx")),
            P(("shard", "ctx", "tensor")),
            P(("shard", "ctx"), "tensor"),
            P("tensor", ("shard", "ctx")),
            P("tensor", ("shard", "ctx")),
            P(("shard", "ctx", "tensor")),
        ),
        check_vma=False,
    )
```
